32 devices in a mesh: users: 8 (over y, x, core), hist: 4 (over z).
Axes of the slice: x: 2, y: 2, z: 4, core: 2. Of those that a mesh axis runs over, the one named last changes fastest.
Arguments:
- cand_x: bfloat16 [2048, 512], P(('users', 'hist')), parts along dimension 0, may hold values from -6 to 6
- hist_keys: bfloat16 [16384, 512], P(('users', 'hist')), parts along dimension 0, may hold values from -6 to 6
- hist_values: bfloat16 [16384, 512], P(('users', 'hist')), parts along dimension 0, may hold values from -6 to 6
- key_scale: bfloat16 [16384], P(('users', 'hist')), parts along dimension 0, may hold values from 0.5 to 2
- hist_len: int32 [8], P('users'), parts along dimension 0, may hold values from 512 to 2048
- cand_limit: int32 [2048], P('users'), parts along dimension 0, may hold values from 1 to 2048
- ln_gain: float32 [512], replicated, may hold values from 0.1 to 1.9
- w_qu: bfloat16 [512, 1024], replicated, may hold values from -0.25 to 0.25
- w_out: bfloat16 [512, 512], replicated, may hold values from -0.25 to 0.25
Outputs:
- scored: bfloat16 [2048, 512], P(('users', 'hist')), parts along dimension 0
The draws below stay inside these ranges and needn't reach their ends.
There are 8 independent parts, one for each index of `users`. The reference program is written for one: setup_inputs(seed, part) draws one part's arguments, and reference() takes and returns one part's arrays. A program takes and returns all parts, laid end to end along the dimension named above; an argument that names none is the same for every part. Nothing has to cross between parts.
All inputs are finite; a program needn't handle non-finite values.
Results may differ from the reference program's by a relative error of at most 0.0058.
Values may be sent and summed in bfloat16 or wider, within the bound.
A program may use at most 64 MiB of HBM per device.

```python
import math
import jax
import jax.numpy as jnp
from jax import lax

D = 512
HEADS = 8
CAND_DEV = 64
NC = 256
HIST = 2048


def touch_ends(result, stream_key, low, largest):
    shape = result.shape
    index_at = [jax.random.randint(jax.random.fold_in(stream_key, axis), (), 0, shape[axis]) for axis in range(len(shape))]
    result = result.at[tuple(index_at)].set(low)
    longest = shape.index(max(shape))
    index_at[longest] = (index_at[longest] + 1) % shape[longest]
    return result.at[tuple(index_at)].set(largest)


def levels(rng, shape, pieces, smallest, top_value):
    factor_of = 1.0
    for position, shards_of in pieces:
        heights = jax.random.uniform(jax.random.fold_in(jax.random.fold_in(rng, 6), position), (shards_of,), jnp.float32, smallest / len(pieces), top_value / len(pieces))
        factor_of = factor_of * jnp.repeat(jnp.exp(heights), shape[position] // shards_of).reshape((-1,) + (1,) * (len(shape) - 1 - position))
    return factor_of


def noise(rng, extent, deviation, reach, pieces=(), held_as=jnp.bfloat16):
    level = levels(rng, extent, pieces, -0.22, 0.18) if pieces else 1.0
    array = jax.random.normal(rng, extent, jnp.float32) * deviation * level
    return jnp.minimum(jnp.maximum(array, -reach), reach).astype(held_as)


def setup_inputs(seed: int = 0, part: int = 0) -> dict:
    arg_keys = jax.random.split(jax.random.key(seed), 10)
    part_splits = jax.random.split(jax.random.fold_in(arg_keys[9], part), 10)
    cand_x = noise(part_splits[0], (NC, D), 1.0, 6.0, ((0, 4),))
    hist_keys = noise(part_splits[1], (HIST, D), 1.0, 6.0, ((0, 4),))
    hist_values = noise(part_splits[2], (HIST, D), 1.0, 6.0, ((0, 4),))
    key_scale = jnp.clip(jnp.exp(math.log(2.0) - 1.3862944 * jax.random.uniform(part_splits[3], (HIST,), jnp.float32) ** levels(part_splits[3], (HIST,), ((0, 4),), -0.2, 0.2)), 0.5, 2.0).astype(jnp.bfloat16)
    hist_len = jax.random.randint(part_splits[4], (1,), HIST // 4, HIST + 1).astype(jnp.int32)
    cand_limit = touch_ends(jax.random.randint(part_splits[5], (NC,), 1, HIST + 1), jax.random.fold_in(part_splits[5], 1), 1, HIST).astype(jnp.int32)
    ln_gain = jnp.clip(1.0 + 0.18 * jax.random.normal(arg_keys[6], (D,), jnp.float32), 0.1, 1.9)
    w_qu = noise(arg_keys[7], (D, 2 * D), D ** -0.5, 0.25)
    w_out = noise(arg_keys[8], (D, D), D ** -0.5, 0.25)
    return dict(cand_x=cand_x, hist_keys=hist_keys, hist_values=hist_values, key_scale=key_scale, hist_len=hist_len, cand_limit=cand_limit, ln_gain=ln_gain, w_qu=w_qu, w_out=w_out)


def row_norm(values):
    center = lax.optimization_barrier(jnp.mean(values, axis=-1, keepdims=True))
    spread = lax.optimization_barrier(jnp.mean((values - center) ** 2, axis=-1, keepdims=True))
    return (values - center) / jnp.sqrt(spread + 1e-05)

def attend(query_rows, history_limits, key_rows, value_rows, scale_rows, offset_pos):
    count = query_rows.shape[0]
    length = key_rows.shape[0]
    width = query_rows.shape[1]
    head_size = width // HEADS
    query_head_blocks = query_rows.reshape(count, HEADS, head_size)
    key_head_blocks = key_rows.reshape(length, HEADS, head_size)
    value_head_blocks = value_rows.reshape(length, HEADS, head_size)
    attention_scores = jnp.einsum('ufe,yfe->fuy', query_head_blocks, key_head_blocks, preferred_element_type=jnp.float32)
    factor = scale_rows.astype(jnp.float32) / jnp.sqrt(jnp.float32(head_size))
    attention_scores = attention_scores * factor[None, None, :]
    positions = offset_pos + jnp.arange(length, dtype=jnp.int32)
    visible = positions[None, :] < history_limits[:, None]
    weight_matrices = jnp.where(visible[None], jax.nn.silu(attention_scores), 0.0).astype(jnp.bfloat16)
    summed_output = jnp.einsum('apn,naf->paf', weight_matrices, value_head_blocks, preferred_element_type=jnp.float32)
    return summed_output.reshape(count, width)

def reference(cand_x, hist_keys, hist_values, key_scale, hist_len, cand_limit, ln_gain, w_qu, w_out):
    inputs32 = cand_x.astype(jnp.float32)
    normed = (row_norm(inputs32) * ln_gain).astype(jnp.bfloat16)
    projected = jax.nn.silu(jnp.dot(normed, w_qu, preferred_element_type=jnp.float32))
    query_vectors = projected[:, :D].astype(jnp.bfloat16)
    gating = projected[:, D:]
    history_limits = jnp.minimum(cand_limit, hist_len[0]).astype(jnp.int32)
    blocks = NC // CAND_DEV

    def one_block(couple):
        return attend(couple[0], couple[1], hist_keys, hist_values, key_scale, jnp.int32(0))
    attended = lax.map(one_block, (query_vectors.reshape(blocks, CAND_DEV, D), history_limits.reshape(blocks, CAND_DEV)))
    attended = attended.reshape(NC, D)
    mixed = (row_norm(attended) * gating).astype(jnp.bfloat16)
    return (inputs32 + jnp.dot(mixed, w_out, preferred_element_type=jnp.float32)).astype(jnp.bfloat16)
```

```python
import functools

import jax
import jax.numpy as jnp
from jax import lax
from jax.experimental import pallas as pl
from jax.experimental.pallas import tpu as pltpu
from jax.sharding import PartitionSpec as P

HEADS = 8
GROUP = 4
LANES = 128
PIECES = 2
MESH = pl.DeviceIdType.MESH
NONE = -1


def plan_of(count):
    if count == 4:
        return dict(
            hello=[[3, 1], [0, 2], [0, 1], [2]],
            ready=[[], [], [3], [0]],
            direct=[[(2, 0, False), (3, 0, True), (1, 2, False)], [(2, 0, False), (0, 0, False)], [(3, 0, False), (1, 0, False)], [(0, 0, False), (2, 1, True)]],
            order=[[1, 3, 2], [2, 0, 3], [1, 0, 3], [2, 0, 1]],
            relay=[{3: 1}, {2: 0}, {1: 3}, {}],
        )
    others = [[(i + k) % count for k in range(1, count)] for i in range(count)]
    return dict(
        hello=others,
        ready=[[]] * count,
        direct=[[(j, 0, False) for j in row] for row in others],
        order=[row[::-1] for row in others],
        relay=[{}] * count,
    )


def pick(me, choices):
    value = jnp.int32(choices[0])
    for i, choice in enumerate(choices[1:], 1):
        if choice != choices[0]:
            value = jnp.where(me == i, choice, value)
    return value


def half_silu(half):
    return half + half * jnp.tanh(half)


def row_norm(values):
    center = jnp.mean(values, axis=-1, keepdims=True)
    spread = jnp.mean((values - center) ** 2, axis=-1, keepdims=True)
    return (values - center) / jnp.sqrt(spread + 1e-05)


def kernel(
    count,
    x_hbm, keys_hbm, values_hbm, scale_hbm, len_hbm, limit_hbm, gain_hbm, wqu_hbm, wout_hbm,
    out_ref,
    x_buf, keys_buf, values_buf, scale_buf, len_buf, limit_buf, gain_buf, wqu_buf, wout_buf,
    keys_t, limit_col, got_x, send_sum, got_sum,
    local_sem, xs_sem, xr_sem, fs_sem, ss_sem, sr_sem, ready_sem,
):
    me = lax.axis_index("hist")
    rows, width = x_buf.shape
    length = keys_buf.shape[0]
    head = width // HEADS
    span = GROUP * head
    size = rows // PIECES
    parts = [(i, pl.ds(i * size, size)) for i in range(PIECES)]
    plan = plan_of(count)
    hello, ready, direct, order, relay = (
        plan[name] for name in ("hello", "ready", "direct", "order", "relay")
    )

    def on_some(choices, act):
        if all(choice == NONE for choice in choices):
            return
        chosen = pick(me, choices)
        if NONE in choices:
            pl.when(chosen != NONE)(lambda: act(chosen))
        else:
            act(chosen)

    def column(table, k):
        return [row[k] if k < len(row) else NONE for row in table]

    def longest(table):
        return max(len(row) for row in table)

    def signal(semaphore, device):
        pl.semaphore_signal(
            semaphore, inc=1, device_id={"hist": device}, device_id_type=MESH
        )

    barrier = pltpu.get_barrier_semaphore()
    for k in range(longest(hello)):
        on_some(column(hello, k), lambda device: signal(barrier, device))

    pairs = [
        (x_hbm, x_buf), (limit_hbm, limit_buf), (len_hbm, len_buf), (gain_hbm, gain_buf),
        (scale_hbm, scale_buf), (keys_hbm, keys_buf), (wqu_hbm, wqu_buf),
        (values_hbm, values_buf), (wout_hbm, wout_buf),
    ]
    loads = [
        pltpu.make_async_copy(src, dst, local_sem.at[i]) for i, (src, dst) in enumerate(pairs)
    ]
    for load in loads:
        load.start()
    x_in, limit_in, len_in, gain_in, scale_in, keys_in, wqu_in, values_in, wout_in = loads
    greeted = [sum(i in row for row in hello) for i in range(count)]
    pl.semaphore_wait(barrier, pick(me, greeted))
    for k in range(longest(ready)):
        on_some(column(ready, k), lambda device: signal(ready_sem, device))

    def copy_of(source, target, send_sem, recv_sem, device):
        return pltpu.make_async_remote_copy(
            src_ref=source, dst_ref=target, send_sem=send_sem, recv_sem=recv_sem,
            device_id={"hist": device}, device_id_type=MESH,
        )

    def x_copies(k, device):
        return [
            copy_of(
                x_buf.at[part], got_x.at[me, part], xs_sem.at[k, i], xr_sem.at[me, i], device
            )
            for i, part in parts
        ]

    def relay_copies(k, source, device):
        return [
            copy_of(
                got_x.at[source, part], got_x.at[source, part],
                fs_sem.at[k, i], xr_sem.at[source, i], device,
            )
            for i, part in parts
        ]

    def sum_copies(k, source):
        return [
            copy_of(
                send_sum.at[k, part], got_sum.at[me, part],
                ss_sem.at[k, i], sr_sem.at[me, i], source,
            )
            for i, part in parts
        ]

    def wait_block(buffer, sem, i, source):
        block = buffer.at[source, parts[i][1]]
        copy_of(block, block, xs_sem.at[0, i], sem.at[source, i], source).wait_recv()

    def send_x(stage):
        for k in range(longest(direct)):
            now = [k < len(row) and row[k][1] == stage for row in direct]
            gated = [0 if now[i] and direct[i][k][2] else NONE for i in range(count)]
            on_some(gated, lambda _: pl.semaphore_wait(ready_sem, 1))
            chosen = [direct[i][k][0] if now[i] else NONE for i in range(count)]

            def go(device):
                for copy in x_copies(k, device):
                    copy.start()

            on_some(chosen, go)

    hops = [[relay[i].get(order[i][k], NONE) for i in range(count)] for k in range(count - 1)]

    def hand_on(k, source):
        def act(device):
            for i, copy in enumerate(relay_copies(k, source, device)):
                wait_block(got_x, xr_sem, i, source)
                copy.start()

        on_some(hops[k], act)

    x_in.wait()
    send_x(0)
    limit_in.wait()
    len_in.wait()
    limits = jnp.minimum(
        limit_buf[...].reshape(1, -1), len_buf[...].reshape(1, 1)
    ).astype(jnp.float32)
    limit_col[...] = jnp.broadcast_to(limits, (LANES, limits.shape[1])).T
    gain_in.wait()
    scale_in.wait()
    keys_in.wait()
    keys_t[...] = keys_buf[...].T
    send_x(1)
    gain = gain_buf[...].reshape(1, width)
    factor_row = scale_buf[...].astype(jnp.float32).reshape(1, length) * (0.5 / head**0.5)
    positions = (
        lax.broadcasted_iota(jnp.int32, (rows, length), 1) + me * length
    ).astype(jnp.float32)
    head_of_lane = lax.broadcasted_iota(jnp.int32, (rows, span), 1) // head

    def normed_of(block):
        return (row_norm(block.astype(jnp.float32)) * gain).astype(jnp.bfloat16)

    def attend(normed, first):
        rows = normed.shape[0]
        lane_head = head_of_lane[:rows]
        raw = jnp.dot(normed, wqu_buf[:, :width], preferred_element_type=jnp.float32)
        queries = half_silu(raw * 0.5)
        own_limit = limit_col[pl.ds(pl.multiple_of(first, rows), rows), :]
        own_limit = jnp.concatenate([own_limit] * (length // LANES), axis=1)
        factor = jnp.where(positions[:rows] < own_limit, factor_row, 0.0)
        factor = jnp.concatenate([factor] * GROUP, axis=0)
        parts = []
        for start in range(0, width, span):
            some = queries[:, start : start + span]
            stacked = jnp.concatenate(
                [jnp.where(lane_head == i, some, 0.0) for i in range(GROUP)], axis=0
            ).astype(jnp.bfloat16)
            scores = jnp.dot(
                stacked, keys_t[start : start + span, :], preferred_element_type=jnp.float32
            )
            weights = half_silu(scores * factor).astype(jnp.bfloat16)
            summed = jnp.dot(
                weights, values_buf[:, start : start + span], preferred_element_type=jnp.float32
            )
            part = summed[:rows]
            for i in range(1, GROUP):
                part = jnp.where(lane_head == i, summed[i * rows : (i + 1) * rows], part)
            parts.append(part)
        return jnp.concatenate(parts, axis=1)

    normed = normed_of(x_buf[...])
    wqu_in.wait()
    values_in.wait()
    total = attend(normed, me * rows)
    gating = half_silu(
        0.5 * jnp.dot(normed, wqu_buf[:, width:], preferred_element_type=jnp.float32)
    )
    send_x(2)

    for k in range(count - 1):
        source = pick(me, column(order, k))
        hand_on(k, source)
        copies = sum_copies(k, source)
        for i, part in parts:
            fresh = [0 if hop == NONE else NONE for hop in hops[k]]
            on_some(fresh, lambda _: wait_block(got_x, xr_sem, i, source))
            answer = attend(normed_of(got_x[source, part]), source * rows + part.start)
            send_sum[k, part] = answer.astype(jnp.bfloat16)
            copies[i].start()
        send_x(k + 3)

    wout_in.wait()
    for k in range(count - 1):
        source = pick(me, column(order, k))
        for i, _ in parts:
            wait_block(got_sum, sr_sem, i, source)
        total = total + got_sum[source].astype(jnp.float32)
    mixed = (row_norm(total) * gating).astype(jnp.bfloat16)
    scored = x_buf[...].astype(jnp.float32) + jnp.dot(
        mixed, wout_buf[...], preferred_element_type=jnp.float32
    )
    out_ref[...] = scored.astype(jnp.bfloat16)

    def all_sent(copies):
        for copy in copies:
            copy.wait_send()

    for k in range(count - 1):
        source = pick(me, column(order, k))
        targets = [row[k][0] if k < len(row) else NONE for row in direct]
        on_some(targets, lambda device: all_sent(x_copies(k, device)))
        on_some(hops[k], lambda device: all_sent(relay_copies(k, source, device)))
        all_sent(sum_copies(k, source))


def on_device(*args):
    count = lax.axis_size("hist")
    cand_x, limit = args[0], args[5]
    rows, width = cand_x.shape
    length = args[1].shape[0]
    scratch = [
        pltpu.VMEM(a.shape, a.dtype) for a in args
    ]
    scratch += [
        pltpu.VMEM((width, length), jnp.bfloat16),
        pltpu.VMEM((limit.shape[0], LANES), jnp.float32),
        pltpu.VMEM((count, rows, width), jnp.bfloat16),
        pltpu.VMEM((count - 1, rows, width), jnp.bfloat16),
        pltpu.VMEM((count, rows, width), jnp.bfloat16),
        pltpu.SemaphoreType.DMA((len(args),)),
    ]
    scratch += [pltpu.SemaphoreType.DMA((count, PIECES))] * 5
    scratch += [pltpu.SemaphoreType.REGULAR]
    return pl.pallas_call(
        functools.partial(kernel, count),
        out_shape=pltpu.VMEM((rows, width), jnp.bfloat16),
        in_specs=[pl.BlockSpec(memory_space=pl.ANY)] * len(args),
        out_specs=pl.BlockSpec(memory_space=pltpu.VMEM),
        scratch_shapes=scratch,
        compiler_params=pltpu.CompilerParams(
            collective_id=0, has_side_effects=True, vmem_limit_bytes=60 * 1024 * 1024
        ),
    )(*args)


def solution(mesh):
    both = ("users", "hist")
    in_specs = (
        P(both, None), P(both, None), P(both, None), P(both), P("users"), P("users"),
        P(), P(), P(),
    )
    return jax.shard_map(
        on_device, mesh=mesh, in_specs=in_specs, out_specs=P(both, None), check_vma=False
    )
```

```python
import functools

import jax
import jax.numpy as jnp
from jax import lax
from jax.experimental import pallas as pl
from jax.experimental.pallas import tpu as pltpu
from jax.sharding import PartitionSpec as P

HEADS = 8
GROUP = 4
LANES = 128
PIECES = 2
MESH = pl.DeviceIdType.MESH
NONE = -1


def plan_of(count):
    if count == 4:
        return dict(
            early=[2, 1, 1, 0],
            hello=[[3, 1], [0, 2], [0, 1], [2]],
            ready=[[], [], [3], [0]],
            direct=[[(2, 0, False), (3, 0, True), (1, 2, False)], [(2, 0, False), (0, 0, False)], [(3, 0, False), (1, 0, False)], [(0, 0, False), (2, 1, True)]],
            order=[[1, 3, 2], [2, 0, 3], [0, 1, 3], [2, 0, 1]],
            relay=[[(1, 3, 1)], [(0, 2, 0)], [(0, 1, 3)], []],
        )
    others = [[(i + k) % count for k in range(1, count)] for i in range(count)]
    return dict(
        early=[1] * count,
        hello=others,
        ready=[[]] * count,
        direct=[[(j, 0, False) for j in row] for row in others],
        order=[row[::-1] for row in others],
        relay=[[]] * count,
    )


def pick(me, choices):
    value = jnp.int32(choices[0])
    for i, choice in enumerate(choices[1:], 1):
        if choice != choices[0]:
            value = jnp.where(me == i, choice, value)
    return value


def half_silu(half):
    return half + half * jnp.tanh(half)


def row_norm(values):
    center = jnp.mean(values, axis=-1, keepdims=True)
    spread = jnp.mean((values - center) ** 2, axis=-1, keepdims=True)
    return (values - center) / jnp.sqrt(spread + 1e-05)


def kernel(
    count,
    x_hbm, keys_hbm, values_hbm, scale_hbm, len_hbm, limit_hbm, gain_hbm, wqu_hbm, wout_hbm,
    out_ref,
    x_buf, keys_buf, values_buf, scale_buf, len_buf, limit_buf, gain_buf, wqu_buf, wout_buf,
    keys_t, limit_col, own_q, some_q, got_x, send_sum, got_sum,
    local_sem, xs_sem, xr_sem, fs_sem, ss_sem, sr_sem, ready_sem,
):
    me = lax.axis_index("hist")
    rows, width = x_buf.shape
    length = keys_buf.shape[0]
    head = width // HEADS
    span = GROUP * head
    size = rows // PIECES
    parts = [(i, pl.ds(i * size, size)) for i in range(PIECES)]
    plan = plan_of(count)
    raw = [stage < 2 for stage in plan["early"]]
    early, hello, ready, direct, order, relay = (
        plan[name] for name in ("early", "hello", "ready", "direct", "order", "relay")
    )

    def on_some(choices, act):
        if all(choice == NONE for choice in choices):
            return
        chosen = pick(me, choices)
        if NONE in choices:
            pl.when(chosen != NONE)(lambda: act(chosen))
        else:
            act(chosen)

    def column(table, k):
        return [row[k] if k < len(row) else NONE for row in table]

    def longest(table):
        return max(len(row) for row in table)

    def signal(semaphore, device):
        pl.semaphore_signal(
            semaphore, inc=1, device_id={"hist": device}, device_id_type=MESH
        )

    barrier = pltpu.get_barrier_semaphore()
    for k in range(longest(hello)):
        on_some(column(hello, k), lambda device: signal(barrier, device))

    def copy_of(source, target, send_sem, recv_sem, device):
        return pltpu.make_async_remote_copy(
            src_ref=source, dst_ref=target, send_sem=send_sem, recv_sem=recv_sem,
            device_id={"hist": device}, device_id_type=MESH,
        )

    def x_copies(k, device, block=own_q):
        return [
            copy_of(
                block.at[part], got_x.at[me, part], xs_sem.at[k, i], xr_sem.at[me, i], device
            )
            for i, part in parts
        ]

    def relay_copies(k, source, device):
        return [
            copy_of(
                got_x.at[source, part], got_x.at[source, part],
                fs_sem.at[k, i], xr_sem.at[source, i], device,
            )
            for i, part in parts
        ]

    def sum_copies(k, source):
        return [
            copy_of(
                send_sum.at[k, part], got_sum.at[me, part],
                ss_sem.at[k, i], sr_sem.at[me, i], source,
            )
            for i, part in parts
        ]

    def wait_block(buffer, sem, i, source):
        block = buffer.at[source, parts[i][1]]
        copy_of(block, block, xs_sem.at[0, i], sem.at[source, i], source).wait_recv()

    def send_x(stage):
        for k in range(longest(direct)):
            now = [k < len(row) and row[k][1] == stage for row in direct]
            gated = [0 if now[i] and direct[i][k][2] else NONE for i in range(count)]
            on_some(gated, lambda _: pl.semaphore_wait(ready_sem, 1))
            for block, is_raw in ((x_hbm, True), (own_q, False)):
                chosen = [
                    direct[i][k][0] if now[i] and raw[i] == is_raw else NONE for i in range(count)
                ]

                def go(device):
                    for copy in x_copies(k, device, block):
                        copy.start()

                on_some(chosen, go)

    def hand_on(k, act):
        for r in range(longest(relay)):
            now = [r < len(row) and row[r][0] == k for row in relay]
            sources = [relay[i][r][1] if now[i] else NONE for i in range(count)]
            device = pick(me, [relay[i][r][2] if now[i] else 0 for i in range(count)])
            on_some(sources, lambda source: act(source, relay_copies(r, source, device)))

    def receive_and_start(source, copies):
        for i, copy in enumerate(copies):
            wait_block(got_x, xr_sem, i, source)
            copy.start()

    def begin(when):
        @pl.when(pick(me, early) == when)
        def _():
            greeted = [sum(i in row for row in hello) for i in range(count)]
            pl.semaphore_wait(barrier, pick(me, greeted))
            for k in range(longest(ready)):
                on_some(column(ready, k), lambda device: signal(ready_sem, device))
            send_x(0)

    begin(0)
    pairs = [
        (x_hbm, x_buf), (gain_hbm, gain_buf), (wqu_hbm, wqu_buf), (limit_hbm, limit_buf),
        (len_hbm, len_buf), (scale_hbm, scale_buf), (keys_hbm, keys_buf), (values_hbm, values_buf), (wout_hbm, wout_buf),
    ]
    loads = [
        pltpu.make_async_copy(src, dst, local_sem.at[i]) for i, (src, dst) in enumerate(pairs)
    ]
    for load in loads:
        load.start()
    x_in, gain_in, wqu_in, limit_in, len_in, scale_in, keys_in, values_in, wout_in = loads
    begin(1)

    x_in.wait()
    gain_in.wait()
    wqu_in.wait()
    gain = gain_buf[...].reshape(1, width)

    def normed_of(block):
        return (row_norm(block.astype(jnp.float32)) * gain).astype(jnp.bfloat16)

    def queries_of(normed):
        projected = jnp.dot(normed, wqu_buf[:, :width], preferred_element_type=jnp.float32)
        return half_silu(projected * 0.5).astype(jnp.bfloat16)

    normed = normed_of(x_buf[...])
    own_q[...] = queries_of(normed)
    begin(2)

    limit_in.wait()
    len_in.wait()
    limits = jnp.minimum(
        limit_buf[...].reshape(1, -1), len_buf[...].reshape(1, 1)
    ).astype(jnp.float32)
    limit_col[...] = jnp.broadcast_to(limits, (LANES, limits.shape[1])).T
    scale_in.wait()
    keys_in.wait()
    keys_t[...] = keys_buf[...].T
    send_x(1)
    factor_row = scale_buf[...].astype(jnp.float32).reshape(1, length) * (0.5 / head**0.5)
    positions = (
        lax.broadcasted_iota(jnp.int32, (rows, length), 1) + me * length
    ).astype(jnp.float32)
    head_of_lane = lax.broadcasted_iota(jnp.int32, (rows, span), 1) // head

    def attend(queries, first):
        rows = queries.shape[0]
        queries = queries.astype(jnp.float32)
        lane_head = head_of_lane[:rows]
        own_limit = limit_col[pl.ds(pl.multiple_of(first, rows), rows), :]
        own_limit = jnp.concatenate([own_limit] * (length // LANES), axis=1)
        factor = jnp.where(positions[:rows] < own_limit, factor_row, 0.0)
        factor = jnp.concatenate([factor] * GROUP, axis=0)
        parts = []
        for start in range(0, width, span):
            some = queries[:, start : start + span]
            stacked = jnp.concatenate(
                [jnp.where(lane_head == i, some, 0.0) for i in range(GROUP)], axis=0
            ).astype(jnp.bfloat16)
            scores = jnp.dot(
                stacked, keys_t[start : start + span, :], preferred_element_type=jnp.float32
            )
            weights = half_silu(scores * factor).astype(jnp.bfloat16)
            summed = jnp.dot(
                weights, values_buf[:, start : start + span], preferred_element_type=jnp.float32
            )
            part = summed[:rows]
            for i in range(1, GROUP):
                part = jnp.where(lane_head == i, summed[i * rows : (i + 1) * rows], part)
            parts.append(part)
        return jnp.concatenate(parts, axis=1)

    values_in.wait()
    total = attend(own_q[...], me * rows)
    gating = half_silu(
        0.5 * jnp.dot(normed, wqu_buf[:, width:], preferred_element_type=jnp.float32)
    )
    send_x(2)

    def queries_from(k, source, part):
        flags = [int(raw[order[i][k]]) for i in range(count)]
        if not any(flags):
            return got_x[source, part]
        if all(flags):
            return queries_of(normed_of(got_x[source, part]))
        flag = pick(me, flags)

        @pl.when(flag == 1)
        def _():
            some_q[...] = queries_of(normed_of(got_x[source, part]))

        @pl.when(flag == 0)
        def _():
            some_q[...] = got_x[source, part]

        return some_q[...]

    for k in range(count - 1):
        source = pick(me, column(order, k))
        hand_on(k, receive_and_start)
        copies = sum_copies(k, source)
        handed = [{row[1] for row in rows_} for rows_ in relay]
        fresh = [NONE if order[i][k] in handed[i] else 0 for i in range(count)]
        for i, part in parts:
            on_some(fresh, lambda _: wait_block(got_x, xr_sem, i, source))
            answer = attend(queries_from(k, source, part), source * rows + part.start)
            send_sum[k, part] = answer.astype(jnp.bfloat16)
            copies[i].start()
        send_x(k + 3)

    wout_in.wait()
    for i, part in parts:
        at = slice(part.start, part.start + size)
        summed = total[at]
        for k in range(count - 1):
            source = pick(me, column(order, k))
            wait_block(got_sum, sr_sem, i, source)
            summed = summed + got_sum[source, part].astype(jnp.float32)
        mixed = (row_norm(summed) * gating[at]).astype(jnp.bfloat16)
        scored = x_buf[part].astype(jnp.float32) + jnp.dot(
            mixed, wout_buf[...], preferred_element_type=jnp.float32
        )
        out_ref[part] = scored.astype(jnp.bfloat16)

    def all_sent(copies):
        for copy in copies:
            copy.wait_send()

    for k in range(count - 1):
        source = pick(me, column(order, k))
        targets = [row[k][0] if k < len(row) else NONE for row in direct]
        on_some(targets, lambda device: all_sent(x_copies(k, device)))
        hand_on(k, lambda _, copies: all_sent(copies))
        all_sent(sum_copies(k, source))


def on_device(*args):
    count = lax.axis_size("hist")
    cand_x, limit = args[0], args[5]
    rows, width = cand_x.shape
    length = args[1].shape[0]
    scratch = [
        pltpu.VMEM(a.shape, a.dtype) for a in args
    ]
    scratch += [
        pltpu.VMEM((width, length), jnp.bfloat16),
        pltpu.VMEM((limit.shape[0], LANES), jnp.float32),
        pltpu.VMEM((rows, width), jnp.bfloat16),
        pltpu.VMEM((rows // PIECES, width), jnp.bfloat16),
        pltpu.VMEM((count, rows, width), jnp.bfloat16),
        pltpu.VMEM((count - 1, rows, width), jnp.bfloat16),
        pltpu.VMEM((count, rows, width), jnp.bfloat16),
        pltpu.SemaphoreType.DMA((len(args),)),
    ]
    scratch += [pltpu.SemaphoreType.DMA((count, PIECES))] * 5
    scratch += [pltpu.SemaphoreType.REGULAR]
    return pl.pallas_call(
        functools.partial(kernel, count),
        out_shape=pltpu.VMEM((rows, width), jnp.bfloat16),
        in_specs=[pl.BlockSpec(memory_space=pl.ANY)] * len(args),
        out_specs=pl.BlockSpec(memory_space=pltpu.VMEM),
        scratch_shapes=scratch,
        compiler_params=pltpu.CompilerParams(
            collective_id=0, has_side_effects=True, vmem_limit_bytes=60 * 1024 * 1024
        ),
    )(*args)


def solution(mesh):
    both = ("users", "hist")
    in_specs = (
        P(both, None), P(both, None), P(both, None), P(both), P("users"), P("users"),
        P(), P(), P(),
    )
    return jax.shard_map(
        on_device, mesh=mesh, in_specs=in_specs, out_specs=P(both, None), check_vma=False
    )
```

```python
import functools

import jax
import jax.numpy as jnp
from jax import lax
from jax.experimental import pallas as pl
from jax.experimental.pallas import tpu as pltpu
from jax.sharding import PartitionSpec as P

HEADS = 8
GROUP = 4
LANES = 128
PIECES = 2
MESH = pl.DeviceIdType.MESH
NONE = -1


def plan_of(count):
    if count == 4:
        return dict(
            early=[2, 1, 1, 0],
            hello=[[3, 1], [2, 3], [0, 3], []],
            ready=[[], [0], [1], [0, 2, 1]],
            direct=[[(1, -1, True), (2, 0, False), (3, 0, True)], [(0, 0, False), (2, 0, True), (3, 1, True)], [(1, 0, False), (3, 1, True)], [(0, 0, False), (2, 1, False)]],
            order=[[1, 3, 2], [0, 2, 3], [0, 1, 3], [2, 0, 1]],
            relay=[[(1, 3, 1)], [(1, 2, 0)], [], []],
        )
    others = [[(i + k) % count for k in range(1, count)] for i in range(count)]
    return dict(
        early=[1] * count,
        hello=others,
        ready=[[]] * count,
        direct=[[(j, 0, False) for j in row] for row in others],
        order=[row[::-1] for row in others],
        relay=[[]] * count,
    )


def pick(me, choices):
    value = jnp.int32(choices[0])
    for i, choice in enumerate(choices[1:], 1):
        if choice != choices[0]:
            value = jnp.where(me == i, choice, value)
    return value


def half_silu(half):
    return half + half * jnp.tanh(half)


def row_norm(values):
    center = jnp.mean(values, axis=-1, keepdims=True)
    spread = jnp.mean((values - center) ** 2, axis=-1, keepdims=True)
    return (values - center) * lax.rsqrt(spread + 1e-05)


def kernel(
    count,
    x_hbm, keys_hbm, values_hbm, scale_hbm, len_hbm, limit_hbm, gain_hbm, wqu_hbm, wout_hbm,
    out_ref,
    x_buf, keys_buf, values_buf, scale_buf, len_buf, limit_buf, gain_buf, wqu_buf, wout_buf,
    keys_t, limit_col, own_q, some_q, got_x, send_sum, got_sum,
    local_sem, xs_sem, xr_sem, fs_sem, ss_sem, sr_sem, ready_sem,
):
    me = lax.axis_index("hist")
    rows, width = x_buf.shape
    length = keys_buf.shape[0]
    head = width // HEADS
    span = GROUP * head
    size = rows // PIECES
    parts = [(i, pl.ds(i * size, size)) for i in range(PIECES)]
    plan = plan_of(count)
    raw = [stage < 2 for stage in plan["early"]]
    early, hello, ready, direct, order, relay = (
        plan[name] for name in ("early", "hello", "ready", "direct", "order", "relay")
    )

    def on_some(choices, act):
        if all(choice == NONE for choice in choices):
            return
        chosen = pick(me, choices)
        if NONE in choices:
            pl.when(chosen != NONE)(lambda: act(chosen))
        else:
            act(chosen)

    def column(table, k):
        return [row[k] if k < len(row) else NONE for row in table]

    def longest(table):
        return max(len(row) for row in table)

    def signal(semaphore, device):
        pl.semaphore_signal(
            semaphore, inc=1, device_id={"hist": device}, device_id_type=MESH
        )

    barrier = pltpu.get_barrier_semaphore()
    for k in range(longest(hello)):
        on_some(column(hello, k), lambda device: signal(barrier, device))

    def copy_of(source, target, send_sem, recv_sem, device):
        return pltpu.make_async_remote_copy(
            src_ref=source, dst_ref=target, send_sem=send_sem, recv_sem=recv_sem,
            device_id={"hist": device}, device_id_type=MESH,
        )

    def x_copies(k, device, block=own_q):
        return [
            copy_of(
                block.at[part], got_x.at[me, part], xs_sem.at[k, i], xr_sem.at[me, i], device
            )
            for i, part in parts
        ]

    def relay_copies(k, source, device):
        return [
            copy_of(
                got_x.at[source, part], got_x.at[source, part],
                fs_sem.at[k, i], xr_sem.at[source, i], device,
            )
            for i, part in parts
        ]

    def sum_copies(k, source):
        return [
            copy_of(
                send_sum.at[k, part], got_sum.at[me, part],
                ss_sem.at[k, i], sr_sem.at[me, i], source,
            )
            for i, part in parts
        ]

    def wait_block(buffer, sem, i, source):
        block = buffer.at[source, parts[i][1]]
        copy_of(block, block, xs_sem.at[0, i], sem.at[source, i], source).wait_recv()

    def send_x(stage):
        for k in range(longest(direct)):
            now = [k < len(row) and row[k][1] == stage for row in direct]
            gated = [direct[i][k][0] if now[i] and direct[i][k][2] else NONE for i in range(count)]
            on_some(gated, lambda device: pl.semaphore_wait(ready_sem.at[device], 1))
            for block, is_raw in ((x_hbm, True), (own_q, False)):
                chosen = [
                    direct[i][k][0] if now[i] and raw[i] == is_raw else NONE for i in range(count)
                ]

                def go(device):
                    for copy in x_copies(k, device, block):
                        copy.start()

                on_some(chosen, go)

    def hand_on(k, act):
        for r in range(longest(relay)):
            now = [r < len(row) and row[r][0] == k for row in relay]
            sources = [relay[i][r][1] if now[i] else NONE for i in range(count)]
            device = pick(me, [relay[i][r][2] if now[i] else 0 for i in range(count)])
            on_some(sources, lambda source: act(source, relay_copies(r, source, device)))

    def receive_and_start(source, copies):
        for i, copy in enumerate(copies):
            wait_block(got_x, xr_sem, i, source)
            copy.start()

    def begin(when):
        @pl.when(pick(me, early) == when)
        def _():
            if when > 1:
                send_x(-1)
            greeted = [sum(i in row for row in hello) for i in range(count)]
            pl.semaphore_wait(barrier, pick(me, greeted))
            for k in range(longest(ready)):
                on_some(column(ready, k), lambda device: signal(ready_sem.at[me], device))
            send_x(0)

    begin(0)
    pairs = [
        (x_hbm, x_buf), (gain_hbm, gain_buf), (wqu_hbm, wqu_buf), (limit_hbm, limit_buf),
        (len_hbm, len_buf), (scale_hbm, scale_buf), (keys_hbm, keys_buf), (values_hbm, values_buf), (wout_hbm, wout_buf),
    ]
    loads = [
        pltpu.make_async_copy(src, dst, local_sem.at[i]) for i, (src, dst) in enumerate(pairs)
    ]
    for load in loads:
        load.start()
    x_in, gain_in, wqu_in, limit_in, len_in, scale_in, keys_in, values_in, wout_in = loads
    begin(1)

    x_in.wait()
    gain_in.wait()
    wqu_in.wait()
    gain = gain_buf[...].reshape(1, width)

    def normed_of(block):
        return (row_norm(block.astype(jnp.float32)) * gain).astype(jnp.bfloat16)

    def queries_of(normed):
        projected = jnp.dot(normed, wqu_buf[:, :width], preferred_element_type=jnp.float32)
        return half_silu(projected * 0.5).astype(jnp.bfloat16)

    normed = normed_of(x_buf[...])
    own_q[...] = queries_of(normed)
    begin(2)

    limit_in.wait()
    len_in.wait()
    limits = jnp.minimum(
        limit_buf[...].reshape(1, -1), len_buf[...].reshape(1, 1)
    ).astype(jnp.float32)
    limit_col[...] = jnp.broadcast_to(limits, (LANES, limits.shape[1])).T
    scale_in.wait()
    keys_in.wait()
    keys_t[...] = keys_buf[...].T
    send_x(1)
    factor_row = scale_buf[...].astype(jnp.float32).reshape(1, length) * (0.5 / head**0.5)
    positions = (
        lax.broadcasted_iota(jnp.int32, (rows, length), 1) + me * length
    ).astype(jnp.float32)
    head_of_lane = lax.broadcasted_iota(jnp.int32, (rows, span), 1) // head

    def attend(queries, first):
        rows = queries.shape[0]
        queries = queries.astype(jnp.float32)
        lane_head = head_of_lane[:rows]
        own_limit = limit_col[pl.ds(pl.multiple_of(first, rows), rows), :]
        own_limit = jnp.concatenate([own_limit] * (length // LANES), axis=1)
        factor = jnp.where(positions[:rows] < own_limit, factor_row, 0.0)
        factor = jnp.concatenate([factor] * GROUP, axis=0)
        parts = []
        for start in range(0, width, span):
            some = queries[:, start : start + span]
            stacked = jnp.concatenate(
                [jnp.where(lane_head == i, some, 0.0) for i in range(GROUP)], axis=0
            ).astype(jnp.bfloat16)
            scores = jnp.dot(
                stacked, keys_t[start : start + span, :], preferred_element_type=jnp.float32
            )
            weights = half_silu(scores * factor).astype(jnp.bfloat16)
            summed = jnp.dot(
                weights, values_buf[:, start : start + span], preferred_element_type=jnp.float32
            )
            part = summed[:rows]
            for i in range(1, GROUP):
                part = jnp.where(lane_head == i, summed[i * rows : (i + 1) * rows], part)
            parts.append(part)
        return jnp.concatenate(parts, axis=1)

    values_in.wait()
    total = attend(own_q[...], me * rows)
    gating = half_silu(
        0.5 * jnp.dot(normed, wqu_buf[:, width:], preferred_element_type=jnp.float32)
    )
    begin(3)
    send_x(2)

    def queries_from(k, source, part):
        flags = [int(raw[order[i][k]]) for i in range(count)]
        if not any(flags):
            return got_x[source, part]
        if all(flags):
            return queries_of(normed_of(got_x[source, part]))
        flag = pick(me, flags)

        @pl.when(flag == 1)
        def _():
            some_q[...] = queries_of(normed_of(got_x[source, part]))

        @pl.when(flag == 0)
        def _():
            some_q[...] = got_x[source, part]

        return some_q[...]

    for k in range(count - 1):
        source = pick(me, column(order, k))
        hand_on(k, receive_and_start)
        copies = sum_copies(k, source)
        handed = [{row[1] for row in rows_} for rows_ in relay]
        fresh = [NONE if order[i][k] in handed[i] else 0 for i in range(count)]
        for i, part in parts:
            on_some(fresh, lambda _: wait_block(got_x, xr_sem, i, source))
            answer = attend(queries_from(k, source, part), source * rows + part.start)
            send_sum[k, part] = answer.astype(jnp.bfloat16)
            copies[i].start()
        send_x(k + 3)

    def all_sent(copies):
        for copy in copies:
            copy.wait_send()

    wout_in.wait()
    for k in range(count - 1):
        targets = [row[k][0] if k < len(row) else NONE for row in direct]
        on_some(targets, lambda device: all_sent(x_copies(k, device)))
        hand_on(k, lambda _, copies: all_sent(copies))
    for i, part in parts:
        at = slice(part.start, part.start + size)
        summed = total[at]
        for k in range(count - 1):
            source = pick(me, column(order, k))
            wait_block(got_sum, sr_sem, i, source)
            summed = summed + got_sum[source, part].astype(jnp.float32)
        mixed = (row_norm(summed) * gating[at]).astype(jnp.bfloat16)
        scored = x_buf[part].astype(jnp.float32) + jnp.dot(
            mixed, wout_buf[...], preferred_element_type=jnp.float32
        )
        out_ref[part] = scored.astype(jnp.bfloat16)

    for k in range(count - 1):
        all_sent(sum_copies(k, pick(me, column(order, k))))


def on_device(*args):
    count = lax.axis_size("hist")
    cand_x, limit = args[0], args[5]
    rows, width = cand_x.shape
    length = args[1].shape[0]
    scratch = [
        pltpu.VMEM(a.shape, a.dtype) for a in args
    ]
    scratch += [
        pltpu.VMEM((width, length), jnp.bfloat16),
        pltpu.VMEM((limit.shape[0], LANES), jnp.float32),
        pltpu.VMEM((rows, width), jnp.bfloat16),
        pltpu.VMEM((rows // PIECES, width), jnp.bfloat16),
        pltpu.VMEM((count, rows, width), jnp.bfloat16),
        pltpu.VMEM((count - 1, rows, width), jnp.bfloat16),
        pltpu.VMEM((count, rows, width), jnp.bfloat16),
        pltpu.SemaphoreType.DMA((len(args),)),
    ]
    scratch += [pltpu.SemaphoreType.DMA((count, PIECES))] * 5
    scratch += [pltpu.SemaphoreType.REGULAR((count,))]
    return pl.pallas_call(
        functools.partial(kernel, count),
        out_shape=pltpu.VMEM((rows, width), jnp.bfloat16),
        in_specs=[pl.BlockSpec(memory_space=pl.ANY)] * len(args),
        out_specs=pl.BlockSpec(memory_space=pltpu.VMEM),
        scratch_shapes=scratch,
        compiler_params=pltpu.CompilerParams(
            collective_id=0, has_side_effects=True, vmem_limit_bytes=60 * 1024 * 1024
        ),
    )(*args)


def solution(mesh):
    both = ("users", "hist")
    in_specs = (
        P(both, None), P(both, None), P(both, None), P(both), P("users"), P("users"),
        P(), P(), P(),
    )
    return jax.shard_map(
        on_device, mesh=mesh, in_specs=in_specs, out_specs=P(both, None), check_vma=False
    )
```

```python
import functools

import jax
import jax.numpy as jnp
from jax import lax
from jax.experimental import pallas as pl
from jax.experimental.pallas import tpu as pltpu
from jax.sharding import PartitionSpec as P

HEADS = 8
GROUP = 4
LANES = 128
PIECES = 2
MESH = pl.DeviceIdType.MESH
NONE = -1


def plan_of(count):
    if count == 4:
        return dict(
            early=[2, 4, 4, 0],
            hello=[[3, 1], [2, 3], [0, 3], []],
            ready=[[], [0], [1], [0, 2, 1]],
            direct=[[(1, -1, True), (2, 0, False), (3, 0, True)], [(0, 0, False), (2, 0, True), (3, 1, True)], [(1, 0, False), (3, 0, True)], [(0, 0, False), (2, 1, False)]],
            order=[[1, 3, 2], [0, 2, 3], [0, 1, 3], [2, 0, 1]],
            relay=[[(1, 3, 1)], [(1, 2, 0)], [], []],
        )
    others = [[(i + k) % count for k in range(1, count)] for i in range(count)]
    return dict(
        early=[1] * count,
        hello=others,
        ready=[[]] * count,
        direct=[[(j, 0, False) for j in row] for row in others],
        order=[row[::-1] for row in others],
        relay=[[]] * count,
    )


def pick(me, choices):
    value = jnp.int32(choices[0])
    for i, choice in enumerate(choices[1:], 1):
        if choice != choices[0]:
            value = jnp.where(me == i, choice, value)
    return value


def half_silu(half):
    return half + half * jnp.tanh(half)


def row_norm(values):
    center = jnp.mean(values, axis=-1, keepdims=True)
    spread = jnp.mean((values - center) ** 2, axis=-1, keepdims=True)
    return (values - center) * lax.rsqrt(spread + 1e-05)


def kernel(
    count,
    x_hbm, keys_hbm, values_hbm, scale_hbm, len_hbm, limit_hbm, gain_hbm, wqu_hbm, wout_hbm,
    out_ref,
    x_buf, keys_buf, values_buf, scale_buf, len_buf, limit_buf, gain_buf, wqu_buf, wout_buf,
    keys_t, limit_col, own_q, some_q, got_x, send_sum, got_sum,
    local_sem, xs_sem, xr_sem, fs_sem, ss_sem, sr_sem, ready_sem,
):
    me = lax.axis_index("hist")
    rows, width = x_buf.shape
    length = keys_buf.shape[0]
    head = width // HEADS
    span = GROUP * head
    size = rows // PIECES
    parts = [(i, pl.ds(i * size, size)) for i in range(PIECES)]
    plan = plan_of(count)
    raw = [stage < 2 for stage in plan["early"]]
    early, hello, ready, direct, order, relay = (
        plan[name] for name in ("early", "hello", "ready", "direct", "order", "relay")
    )

    def on_some(choices, act):
        if all(choice == NONE for choice in choices):
            return
        chosen = pick(me, choices)
        if NONE in choices:
            pl.when(chosen != NONE)(lambda: act(chosen))
        else:
            act(chosen)

    def column(table, k):
        return [row[k] if k < len(row) else NONE for row in table]

    def longest(table):
        return max(len(row) for row in table)

    def signal(semaphore, device):
        pl.semaphore_signal(
            semaphore, inc=1, device_id={"hist": device}, device_id_type=MESH
        )

    barrier = pltpu.get_barrier_semaphore()
    for k in range(longest(hello)):
        on_some(column(hello, k), lambda device: signal(barrier, device))

    def copy_of(source, target, send_sem, recv_sem, device):
        return pltpu.make_async_remote_copy(
            src_ref=source, dst_ref=target, send_sem=send_sem, recv_sem=recv_sem,
            device_id={"hist": device}, device_id_type=MESH,
        )

    def x_copies(k, device, block=own_q):
        return [
            copy_of(
                block.at[part], got_x.at[me, part], xs_sem.at[k, i], xr_sem.at[me, i], device
            )
            for i, part in parts
        ]

    def relay_copies(k, source, device):
        return [
            copy_of(
                got_x.at[source, part], got_x.at[source, part],
                fs_sem.at[k, i], xr_sem.at[source, i], device,
            )
            for i, part in parts
        ]

    def sum_copies(k, source):
        return [
            copy_of(
                send_sum.at[k, part], got_sum.at[me, part],
                ss_sem.at[k, i], sr_sem.at[me, i], source,
            )
            for i, part in parts
        ]

    def wait_block(buffer, sem, i, source):
        block = buffer.at[source, parts[i][1]]
        copy_of(block, block, xs_sem.at[0, i], sem.at[source, i], source).wait_recv()

    def send_x(stage):
        for k in range(longest(direct)):
            now = [k < len(row) and row[k][1] == stage for row in direct]
            gated = [direct[i][k][0] if now[i] and direct[i][k][2] else NONE for i in range(count)]
            on_some(gated, lambda device: pl.semaphore_wait(ready_sem.at[device], 1))
            for block, is_raw in ((x_hbm, True), (own_q, False)):
                chosen = [
                    direct[i][k][0] if now[i] and raw[i] == is_raw else NONE for i in range(count)
                ]

                def go(device):
                    for copy in x_copies(k, device, block):
                        copy.start()

                on_some(chosen, go)

    def hand_on(k, act):
        for r in range(longest(relay)):
            now = [r < len(row) and row[r][0] == k for row in relay]
            sources = [relay[i][r][1] if now[i] else NONE for i in range(count)]
            device = pick(me, [relay[i][r][2] if now[i] else 0 for i in range(count)])
            on_some(sources, lambda source: act(source, relay_copies(r, source, device)))

    def receive_and_start(source, copies):
        for i, copy in enumerate(copies):
            wait_block(got_x, xr_sem, i, source)
            copy.start()

    def begin(when):
        def greet(_):
            if when > 1:
                send_x(-1)
            greeted = [sum(i in row for row in hello) for i in range(count)]
            pl.semaphore_wait(barrier, pick(me, greeted))
            for k in range(longest(ready)):
                on_some(column(ready, k), lambda device: signal(ready_sem.at[me], device))

        on_some([0 if (1 if at == 4 else at) == when else NONE for at in early], greet)
        on_some(
            [0 if (2 if at == 4 else at) == when else NONE for at in early], lambda _: send_x(0)
        )

    begin(0)
    pairs = [
        (x_hbm, x_buf), (gain_hbm, gain_buf), (wqu_hbm, wqu_buf), (limit_hbm, limit_buf),
        (len_hbm, len_buf), (scale_hbm, scale_buf), (keys_hbm, keys_buf), (values_hbm, values_buf), (wout_hbm, wout_buf),
    ]
    loads = [
        pltpu.make_async_copy(src, dst, local_sem.at[i]) for i, (src, dst) in enumerate(pairs)
    ]
    for load in loads:
        load.start()
    x_in, gain_in, wqu_in, limit_in, len_in, scale_in, keys_in, values_in, wout_in = loads
    begin(1)

    x_in.wait()
    gain_in.wait()
    wqu_in.wait()
    gain = gain_buf[...].reshape(1, width)

    def normed_of(block):
        return (row_norm(block.astype(jnp.float32)) * gain).astype(jnp.bfloat16)

    def queries_of(normed):
        projected = jnp.dot(normed, wqu_buf[:, :width], preferred_element_type=jnp.float32)
        return half_silu(projected * 0.5).astype(jnp.bfloat16)

    normed = normed_of(x_buf[...])
    own_q[...] = queries_of(normed)
    begin(2)

    limit_in.wait()
    len_in.wait()
    limits = jnp.minimum(
        limit_buf[...].reshape(1, -1), len_buf[...].reshape(1, 1)
    ).astype(jnp.float32)
    limit_col[...] = jnp.broadcast_to(limits, (LANES, limits.shape[1])).T
    scale_in.wait()
    keys_in.wait()
    keys_t[...] = keys_buf[...].T
    send_x(1)
    factor_row = scale_buf[...].astype(jnp.float32).reshape(1, length) * (0.5 / head**0.5)
    positions = (
        lax.broadcasted_iota(jnp.int32, (rows, length), 1) + me * length
    ).astype(jnp.float32)
    head_of_lane = lax.broadcasted_iota(jnp.int32, (rows, span), 1) // head

    def attend(queries, first):
        rows = queries.shape[0]
        queries = queries.astype(jnp.float32)
        lane_head = head_of_lane[:rows]
        own_limit = limit_col[pl.ds(pl.multiple_of(first, rows), rows), :]
        own_limit = jnp.concatenate([own_limit] * (length // LANES), axis=1)
        factor = jnp.where(positions[:rows] < own_limit, factor_row, 0.0)
        factor = jnp.concatenate([factor] * GROUP, axis=0)
        parts = []
        for start in range(0, width, span):
            some = queries[:, start : start + span]
            stacked = jnp.concatenate(
                [jnp.where(lane_head == i, some, 0.0) for i in range(GROUP)], axis=0
            ).astype(jnp.bfloat16)
            scores = jnp.dot(
                stacked, keys_t[start : start + span, :], preferred_element_type=jnp.float32
            )
            weights = half_silu(scores * factor).astype(jnp.bfloat16)
            summed = jnp.dot(
                weights, values_buf[:, start : start + span], preferred_element_type=jnp.float32
            )
            part = summed[:rows]
            for i in range(1, GROUP):
                part = jnp.where(lane_head == i, summed[i * rows : (i + 1) * rows], part)
            parts.append(part)
        return jnp.concatenate(parts, axis=1)

    values_in.wait()
    total = attend(own_q[...], me * rows)
    gating = half_silu(
        0.5 * jnp.dot(normed, wqu_buf[:, width:], preferred_element_type=jnp.float32)
    )
    begin(3)
    send_x(2)

    def queries_from(k, source, part):
        flags = [int(raw[order[i][k]]) for i in range(count)]
        if not any(flags):
            return got_x[source, part]
        if all(flags):
            return queries_of(normed_of(got_x[source, part]))
        flag = pick(me, flags)

        @pl.when(flag == 1)
        def _():
            some_q[...] = queries_of(normed_of(got_x[source, part]))

        @pl.when(flag == 0)
        def _():
            some_q[...] = got_x[source, part]

        return some_q[...]

    for k in range(count - 1):
        source = pick(me, column(order, k))
        hand_on(k, receive_and_start)
        copies = sum_copies(k, source)
        handed = [{row[1] for row in rows_} for rows_ in relay]
        fresh = [NONE if order[i][k] in handed[i] else 0 for i in range(count)]
        for i, part in parts:
            on_some(fresh, lambda _: wait_block(got_x, xr_sem, i, source))
            answer = attend(queries_from(k, source, part), source * rows + part.start)
            send_sum[k, part] = answer.astype(jnp.bfloat16)
            copies[i].start()
        send_x(k + 3)

    def all_sent(copies):
        for copy in copies:
            copy.wait_send()

    wout_in.wait()
    for k in range(count - 1):
        targets = [row[k][0] if k < len(row) else NONE for row in direct]
        on_some(targets, lambda device: all_sent(x_copies(k, device)))
        hand_on(k, lambda _, copies: all_sent(copies))
    for i, part in parts:
        at = slice(part.start, part.start + size)
        summed = total[at]
        for k in range(count - 1):
            source = pick(me, column(order, k))
            wait_block(got_sum, sr_sem, i, source)
            summed = summed + got_sum[source, part].astype(jnp.float32)
        mixed = (row_norm(summed) * gating[at]).astype(jnp.bfloat16)
        scored = x_buf[part].astype(jnp.float32) + jnp.dot(
            mixed, wout_buf[...], preferred_element_type=jnp.float32
        )
        out_ref[part] = scored.astype(jnp.bfloat16)

    for k in range(count - 1):
        all_sent(sum_copies(k, pick(me, column(order, k))))


def on_device(*args):
    count = lax.axis_size("hist")
    cand_x, limit = args[0], args[5]
    rows, width = cand_x.shape
    length = args[1].shape[0]
    scratch = [
        pltpu.VMEM(a.shape, a.dtype) for a in args
    ]
    scratch += [
        pltpu.VMEM((width, length), jnp.bfloat16),
        pltpu.VMEM((limit.shape[0], LANES), jnp.float32),
        pltpu.VMEM((rows, width), jnp.bfloat16),
        pltpu.VMEM((rows // PIECES, width), jnp.bfloat16),
        pltpu.VMEM((count, rows, width), jnp.bfloat16),
        pltpu.VMEM((count - 1, rows, width), jnp.bfloat16),
        pltpu.VMEM((count, rows, width), jnp.bfloat16),
        pltpu.SemaphoreType.DMA((len(args),)),
    ]
    scratch += [pltpu.SemaphoreType.DMA((count, PIECES))] * 5
    scratch += [pltpu.SemaphoreType.REGULAR((count,))]
    return pl.pallas_call(
        functools.partial(kernel, count),
        out_shape=pltpu.VMEM((rows, width), jnp.bfloat16),
        in_specs=[pl.BlockSpec(memory_space=pl.ANY)] * len(args),
        out_specs=pl.BlockSpec(memory_space=pltpu.VMEM),
        scratch_shapes=scratch,
        compiler_params=pltpu.CompilerParams(
            collective_id=0, has_side_effects=True, vmem_limit_bytes=60 * 1024 * 1024
        ),
    )(*args)


def solution(mesh):
    both = ("users", "hist")
    in_specs = (
        P(both, None), P(both, None), P(both, None), P(both), P("users"), P("users"),
        P(), P(), P(),
    )
    return jax.shard_map(
        on_device, mesh=mesh, in_specs=in_specs, out_specs=P(both, None), check_vma=False
    )
```

```python
import functools

import jax
import jax.numpy as jnp
from jax import lax
from jax.experimental import pallas as pl
from jax.experimental.pallas import tpu as pltpu
from jax.sharding import PartitionSpec as P

HEADS = 8
GROUP = 4
LANES = 128
PIECES = 2
MESH = pl.DeviceIdType.MESH
NONE = -1


def plan_of(count):
    if count == 4:
        return dict(
            early=[2, 1, 1, 0],
            hello=[[3, 1], [2, 3], [0, 3], []],
            ready=[[], [0], [1], [0, 2, 1]],
            direct=[[(1, -1, True), (2, 0, False), (3, 0, True)], [(0, 0, False), (2, 0, True), (3, 1, True)], [(1, 1, False), (3, 1, True)], [(0, 0, False), (2, 1, False)]],
            order=[[1, 3, 2], [0, 2, 3], [0, 1, 3], [2, 0, 1]],
            relay=[[(1, 3, 1)], [(1, 2, 0)], [], []],
        )
    others = [[(i + k) % count for k in range(1, count)] for i in range(count)]
    return dict(
        early=[1] * count,
        hello=others,
        ready=[[]] * count,
        direct=[[(j, 0, False) for j in row] for row in others],
        order=[row[::-1] for row in others],
        relay=[[]] * count,
    )


def pick(me, choices):
    value = jnp.int32(choices[0])
    for i, choice in enumerate(choices[1:], 1):
        if choice != choices[0]:
            value = jnp.where(me == i, choice, value)
    return value


def half_silu(half):
    return half + half * jnp.tanh(half)


def row_norm(values):
    center = jnp.mean(values, axis=-1, keepdims=True)
    spread = jnp.mean((values - center) ** 2, axis=-1, keepdims=True)
    return (values - center) * lax.rsqrt(spread + 1e-05)


def kernel(
    count,
    x_hbm, keys_hbm, values_hbm, scale_hbm, len_hbm, limit_hbm, gain_hbm, wqu_hbm, wout_hbm,
    out_ref,
    x_buf, keys_buf, values_buf, scale_buf, len_buf, limit_buf, gain_buf, wqu_buf, wout_buf,
    keys_t, limit_col, own_q, some_q, got_x, send_sum, got_sum,
    local_sem, xs_sem, xr_sem, fs_sem, ss_sem, sr_sem, ready_sem,
):
    me = lax.axis_index("hist")
    rows, width = x_buf.shape
    length = keys_buf.shape[0]
    head = width // HEADS
    span = GROUP * head
    size = rows // PIECES
    parts = [(i, pl.ds(i * size, size)) for i in range(PIECES)]
    plan = plan_of(count)
    raw = [stage < 2 for stage in plan["early"]]
    early, hello, ready, direct, order, relay = (
        plan[name] for name in ("early", "hello", "ready", "direct", "order", "relay")
    )

    def on_some(choices, act):
        if all(choice == NONE for choice in choices):
            return
        chosen = pick(me, choices)
        if NONE in choices:
            pl.when(chosen != NONE)(lambda: act(chosen))
        else:
            act(chosen)

    def column(table, k):
        return [row[k] if k < len(row) else NONE for row in table]

    def longest(table):
        return max(len(row) for row in table)

    def signal(semaphore, device):
        pl.semaphore_signal(
            semaphore, inc=1, device_id={"hist": device}, device_id_type=MESH
        )

    barrier = pltpu.get_barrier_semaphore()
    for k in range(longest(hello)):
        on_some(column(hello, k), lambda device: signal(barrier, device))

    def copy_of(source, target, send_sem, recv_sem, device):
        return pltpu.make_async_remote_copy(
            src_ref=source, dst_ref=target, send_sem=send_sem, recv_sem=recv_sem,
            device_id={"hist": device}, device_id_type=MESH,
        )

    def x_copies(k, device, block=own_q):
        return [
            copy_of(
                block.at[part], got_x.at[me, part], xs_sem.at[k, i], xr_sem.at[me, i], device
            )
            for i, part in parts
        ]

    def relay_copies(k, source, device):
        return [
            copy_of(
                got_x.at[source, part], got_x.at[source, part],
                fs_sem.at[k, i], xr_sem.at[source, i], device,
            )
            for i, part in parts
        ]

    def sum_copies(k, source):
        return [
            copy_of(
                send_sum.at[k, part], got_sum.at[me, part],
                ss_sem.at[k, i], sr_sem.at[me, i], source,
            )
            for i, part in parts
        ]

    def wait_block(buffer, sem, i, source):
        block = buffer.at[source, parts[i][1]]
        copy_of(block, block, xs_sem.at[0, i], sem.at[source, i], source).wait_recv()

    def send_x(stage):
        for k in range(longest(direct)):
            now = [k < len(row) and row[k][1] == stage for row in direct]
            gated = [direct[i][k][0] if now[i] and direct[i][k][2] else NONE for i in range(count)]
            on_some(gated, lambda device: pl.semaphore_wait(ready_sem.at[device], 1))
            for block, is_raw in ((x_hbm, True), (own_q, False)):
                chosen = [
                    direct[i][k][0] if now[i] and raw[i] == is_raw else NONE for i in range(count)
                ]

                def go(device):
                    for copy in x_copies(k, device, block):
                        copy.start()

                on_some(chosen, go)

    def hand_on(k, act):
        for r in range(longest(relay)):
            now = [r < len(row) and row[r][0] == k for row in relay]
            sources = [relay[i][r][1] if now[i] else NONE for i in range(count)]
            device = pick(me, [relay[i][r][2] if now[i] else 0 for i in range(count)])
            on_some(sources, lambda source: act(source, relay_copies(r, source, device)))

    def receive_and_start(source, copies):
        for i, copy in enumerate(copies):
            wait_block(got_x, xr_sem, i, source)
            copy.start()

    def begin(when):
        @pl.when(pick(me, early) == when)
        def _():
            if when > 1:
                send_x(-1)
            greeted = [sum(i in row for row in hello) for i in range(count)]
            pl.semaphore_wait(barrier, pick(me, greeted))
            for k in range(longest(ready)):
                on_some(column(ready, k), lambda device: signal(ready_sem.at[me], device))
            send_x(0)

    begin(0)
    pairs = [
        (x_hbm, x_buf), (gain_hbm, gain_buf), (wqu_hbm, wqu_buf), (limit_hbm, limit_buf),
        (len_hbm, len_buf), (scale_hbm, scale_buf), (keys_hbm, keys_buf), (values_hbm, values_buf), (wout_hbm, wout_buf),
    ]
    loads = [
        pltpu.make_async_copy(src, dst, local_sem.at[i]) for i, (src, dst) in enumerate(pairs)
    ]
    for load in loads:
        load.start()
    x_in, gain_in, wqu_in, limit_in, len_in, scale_in, keys_in, values_in, wout_in = loads
    begin(1)

    x_in.wait()
    gain_in.wait()
    wqu_in.wait()
    gain = gain_buf[...].reshape(1, width)

    def normed_of(block):
        return (row_norm(block.astype(jnp.float32)) * gain).astype(jnp.bfloat16)

    def queries_of(normed):
        projected = jnp.dot(normed, wqu_buf[:, :width], preferred_element_type=jnp.float32)
        return half_silu(projected * 0.5).astype(jnp.bfloat16)

    normed = normed_of(x_buf[...])
    own_q[...] = queries_of(normed)
    begin(2)

    limit_in.wait()
    len_in.wait()
    limits = jnp.minimum(
        limit_buf[...].reshape(1, -1), len_buf[...].reshape(1, 1)
    ).astype(jnp.float32)
    limit_col[...] = jnp.broadcast_to(limits, (LANES, limits.shape[1])).T
    scale_in.wait()
    keys_in.wait()
    keys_t[...] = keys_buf[...].T
    send_x(1)
    factor_row = scale_buf[...].astype(jnp.float32).reshape(1, length) * (0.5 / head**0.5)
    positions = (
        lax.broadcasted_iota(jnp.int32, (rows, length), 1) + me * length
    ).astype(jnp.float32)
    head_of_lane = lax.broadcasted_iota(jnp.int32, (rows, span), 1) // head

    def attend(queries, first):
        rows = queries.shape[0]
        queries = queries.astype(jnp.float32)
        lane_head = head_of_lane[:rows]
        own_limit = limit_col[pl.ds(pl.multiple_of(first, rows), rows), :]
        own_limit = jnp.concatenate([own_limit] * (length // LANES), axis=1)
        factor = jnp.where(positions[:rows] < own_limit, factor_row, 0.0)
        factor = jnp.concatenate([factor] * GROUP, axis=0)
        parts = []
        for start in range(0, width, span):
            some = queries[:, start : start + span]
            stacked = jnp.concatenate(
                [jnp.where(lane_head == i, some, 0.0) for i in range(GROUP)], axis=0
            ).astype(jnp.bfloat16)
            scores = jnp.dot(
                stacked, keys_t[start : start + span, :], preferred_element_type=jnp.float32
            )
            weights = half_silu(scores * factor).astype(jnp.bfloat16)
            summed = jnp.dot(
                weights, values_buf[:, start : start + span], preferred_element_type=jnp.float32
            )
            part = summed[:rows]
            for i in range(1, GROUP):
                part = jnp.where(lane_head == i, summed[i * rows : (i + 1) * rows], part)
            parts.append(part)
        return jnp.concatenate(parts, axis=1)

    values_in.wait()
    total = attend(own_q[...], me * rows)
    gating = half_silu(
        0.5 * jnp.dot(normed, wqu_buf[:, width:], preferred_element_type=jnp.float32)
    )
    begin(3)
    send_x(2)

    def queries_from(k, source, part):
        flags = [int(raw[order[i][k]]) for i in range(count)]
        if not any(flags):
            return got_x[source, part]
        if all(flags):
            return queries_of(normed_of(got_x[source, part]))
        flag = pick(me, flags)

        @pl.when(flag == 1)
        def _():
            some_q[...] = queries_of(normed_of(got_x[source, part]))

        @pl.when(flag == 0)
        def _():
            some_q[...] = got_x[source, part]

        return some_q[...]

    for k in range(count - 1):
        source = pick(me, column(order, k))
        hand_on(k, receive_and_start)
        copies = sum_copies(k, source)
        handed = [{row[1] for row in rows_} for rows_ in relay]
        fresh = [NONE if order[i][k] in handed[i] else 0 for i in range(count)]
        for i, part in parts:
            on_some(fresh, lambda _: wait_block(got_x, xr_sem, i, source))
            answer = attend(queries_from(k, source, part), source * rows + part.start)
            send_sum[k, part] = answer.astype(jnp.bfloat16)
            copies[i].start()
        send_x(k + 3)

    def all_sent(copies):
        for copy in copies:
            copy.wait_send()

    wout_in.wait()
    for k in range(count - 1):
        targets = [row[k][0] if k < len(row) else NONE for row in direct]
        on_some(targets, lambda device: all_sent(x_copies(k, device)))
        hand_on(k, lambda _, copies: all_sent(copies))
    for i, part in parts:
        at = slice(part.start, part.start + size)
        summed = total[at]
        for k in range(count - 1):
            source = pick(me, column(order, k))
            wait_block(got_sum, sr_sem, i, source)
            summed = summed + got_sum[source, part].astype(jnp.float32)
        mixed = (row_norm(summed) * gating[at]).astype(jnp.bfloat16)
        scored = x_buf[part].astype(jnp.float32) + jnp.dot(
            mixed, wout_buf[...], preferred_element_type=jnp.float32
        )
        out_ref[part] = scored.astype(jnp.bfloat16)

    for k in range(count - 1):
        all_sent(sum_copies(k, pick(me, column(order, k))))


def on_device(*args):
    count = lax.axis_size("hist")
    cand_x, limit = args[0], args[5]
    rows, width = cand_x.shape
    length = args[1].shape[0]
    scratch = [
        pltpu.VMEM(a.shape, a.dtype) for a in args
    ]
    scratch += [
        pltpu.VMEM((width, length), jnp.bfloat16),
        pltpu.VMEM((limit.shape[0], LANES), jnp.float32),
        pltpu.VMEM((rows, width), jnp.bfloat16),
        pltpu.VMEM((rows // PIECES, width), jnp.bfloat16),
        pltpu.VMEM((count, rows, width), jnp.bfloat16),
        pltpu.VMEM((count - 1, rows, width), jnp.bfloat16),
        pltpu.VMEM((count, rows, width), jnp.bfloat16),
        pltpu.SemaphoreType.DMA((len(args),)),
    ]
    scratch += [pltpu.SemaphoreType.DMA((count, PIECES))] * 5
    scratch += [pltpu.SemaphoreType.REGULAR((count,))]
    return pl.pallas_call(
        functools.partial(kernel, count),
        out_shape=pltpu.VMEM((rows, width), jnp.bfloat16),
        in_specs=[pl.BlockSpec(memory_space=pl.ANY)] * len(args),
        out_specs=pl.BlockSpec(memory_space=pltpu.VMEM),
        scratch_shapes=scratch,
        compiler_params=pltpu.CompilerParams(
            collective_id=0, has_side_effects=True, vmem_limit_bytes=60 * 1024 * 1024
        ),
    )(*args)


def solution(mesh):
    both = ("users", "hist")
    in_specs = (
        P(both, None), P(both, None), P(both, None), P(both), P("users"), P("users"),
        P(), P(), P(),
    )
    return jax.shard_map(
        on_device, mesh=mesh, in_specs=in_specs, out_specs=P(both, None), check_vma=False
    )
```
